32 devices in a mesh: tile: 4 (over z), text: 8 (over y, x, core).
Axes of the slice: x: 2, y: 2, z: 4, core: 2. Of those that a mesh axis runs over, the one named last changes fastest.
Arguments:
- grad_seq: bfloat16 [2560, 8192], P('text', 'tile'), may hold values from -6 to 6
- positions: int32 [2560], replicated, may hold values from 0 to 2559, each once
- pre_act: bfloat16 [2560, 5120], P('tile', 'text'), may hold values from -6 to 6
- w_out: bfloat16 [5120, 8192], P('text', 'tile'), may hold values from -0.078125 to 0.078125
Outputs:
- grad_pre: float32 [2560, 5120], P('tile', 'text')
- grad_w_out: float32 [5120, 8192], P('text', 'tile')
- grad_bias: float32 [8192], P('tile')
The draws below stay inside these ranges and needn't reach their ends.
Inputs may be any that keep to these rules, and one draw needn't show every extreme that they name: positions names every place 0 to 2559 once.
All inputs are finite; a program needn't handle non-finite values.
Results may differ from the reference program's by a relative error of at most 0.003.
Values may be sent and summed in bfloat16 or wider, within the bound.
A program may use at most 128 MiB of HBM per device.

```python
import jax
import jax.numpy as jnp
from jax import lax

DM = 5120
OUT = 8192
SLOTS = 2560
N_TILE = 4


def spiked(array, rng, source, target, blocks, factor):
    owner, partner = [(jnp.arange(array.shape[position]) // (array.shape[position] // blocks)).reshape([-1 if axis == position else 1 for axis in range(array.ndim)]) for position in (source, target)]
    chosen = jax.random.permutation(rng, blocks)[partner]
    strong = (owner == chosen) | (owner == (partner + blocks // 2) % blocks)
    return jnp.where(strong, factor * array, array)


def steps_of(rng, dims, pieces, least, high):
    loudness = 1.0
    for dim, parts in pieces:
        draws = jax.random.uniform(jax.random.fold_in(jax.random.fold_in(rng, 6), dim), (parts,), jnp.float32, least / len(pieces), high / len(pieces))
        loudness = loudness * jnp.repeat(jnp.exp(draws), dims[dim] // parts).reshape((-1,) + (1,) * (len(dims) - 1 - dim))
    return loudness


def normal_values(key, extent, scale, bound, cuts=(), kind=jnp.bfloat16):
    loudness = steps_of(key, extent, cuts, -0.22, 0.18) if cuts else 1.0
    array = jax.random.normal(key, extent, jnp.float32) * scale * loudness
    return jnp.minimum(jnp.maximum(array, -bound), bound).astype(kind)


def noise_with(key, extent, scale, reach, cuts, heavy, held_as=jnp.bfloat16):
    drawn = scale * jax.random.normal(key, extent, jnp.float32)
    if cuts:
        drawn = drawn * steps_of(key, extent, cuts, -0.22, 0.18)
    return jnp.clip(spiked(drawn, jax.random.fold_in(key, 3), *heavy), -reach, reach).astype(held_as)


def setup_inputs(seed: int = 0) -> dict:
    key_list = jax.random.split(jax.random.key(seed), 5)
    return {
        "grad_seq": noise_with(key_list[0], (SLOTS, OUT), 1.0, 6.0, ((0, 8), (1, 4)), (0, 1, 8, 2.0)),
        "positions": jax.random.permutation(key_list[1], SLOTS).astype(jnp.int32),
        "pre_act": normal_values(key_list[2], (SLOTS, DM), 1.0, 6.0, ((0, 4), (1, 8))),
        "w_out": normal_values(key_list[3], (DM, OUT), DM ** -0.5, 0.078125, ((0, 8), (1, 4))),
    }


def gelu_parts(pre):
    value = pre.astype(jnp.float32)
    cdf = 0.5 * (1.0 + jax.scipy.special.erf(value * 0.7071067811865476))
    activated = value * cdf
    slope = cdf + value * jnp.exp(-0.5 * value * value) * 0.3989422804014327
    return activated, slope


def reference(grad_seq, positions, pre_act, w_out):
    slot_grad = jnp.take(grad_seq, positions.astype(jnp.int32), axis=0)
    activated, slope = gelu_parts(pre_act)
    act_bf = activated.astype(jnp.bfloat16)
    width = OUT // N_TILE

    def add_block(total, block_index):
        start = (block_index * width).astype(jnp.int32)
        grad_block = lax.dynamic_slice_in_dim(slot_grad, start, width, 1)
        weight_block = lax.dynamic_slice_in_dim(w_out, start, width, 1)
        partial_term = jnp.dot(grad_block, weight_block.T, preferred_element_type=jnp.float32)
        return total + partial_term, None

    start_total = jnp.zeros((slot_grad.shape[0], w_out.shape[0]), jnp.float32)
    grad_act, _ = lax.scan(add_block, start_total, jnp.arange(N_TILE, dtype=jnp.int32))
    grad_pre = grad_act * slope
    grad_w_out = jnp.dot(act_bf.T, slot_grad, preferred_element_type=jnp.float32)
    grad_bias = jnp.sum(grad_seq.astype(jnp.float32), axis=0)
    return grad_pre, grad_w_out, grad_bias
```

```python
import jax
import jax.numpy as jnp
from jax import lax
from jax.sharding import PartitionSpec as P


def gelu_parts(pre):
    value = pre.astype(jnp.float32)
    cdf = 0.5 * (1.0 + jax.scipy.special.erf(value * 0.7071067811865476))
    activated = value * cdf
    slope = cdf + value * jnp.exp(-0.5 * value * value) * 0.3989422804014327
    return (activated, slope)


def rows_of(table, index):
    return table.at[index].get(mode="promise_in_bounds", unique_indices=True)


def line_sum(term, me, n, rows):
    def mine(block):
        start = jnp.clip(block, 0, n - 1) * rows
        return lax.dynamic_slice_in_dim(term, start, rows, 0).astype(jnp.float32)

    total = mine(me)
    right = left = None
    for step in range(1, n):
        ahead = n - step
        out_right, out_left = mine(me + ahead), mine(me - ahead)
        if right is not None:
            out_right = out_right + right.astype(jnp.float32)
            out_left = out_left + left.astype(jnp.float32)
        hops = range(min(step, n - 1))
        right = lax.ppermute(out_right.astype(jnp.bfloat16), "tile", [(i, i + 1) for i in hops])
        left = lax.ppermute(out_left.astype(jnp.bfloat16), "tile", [(n - 1 - i, n - 2 - i) for i in hops])
    return total + right.astype(jnp.float32) + left.astype(jnp.float32)


def solution(mesh):
    n_tile = mesh.shape["tile"]

    def body(grad_seq, positions, pre_act, w_out):
        local_rows, hidden = pre_act.shape
        slots = positions.shape[0]
        me = lax.axis_index("tile")
        gathered = lax.all_gather(grad_seq, "text", axis=0, tiled=True)

        blocks = [pre_act]
        for shift in range(1, n_tile):
            ring = [(i, (i + shift) % n_tile) for i in range(n_tile)]
            blocks.append(lax.ppermute(pre_act, "tile", ring))
        slot = jnp.arange(slots, dtype=jnp.int32)
        turned = (me - slot // local_rows) % n_tile * local_rows + slot % local_rows
        source = jnp.zeros((slots,), jnp.int32).at[positions].set(
            turned, mode="promise_in_bounds", unique_indices=True)
        act = jnp.concatenate([gelu_parts(b)[0].astype(jnp.bfloat16) for b in blocks], axis=0)
        act_seq = rows_of(act, source)
        slope = gelu_parts(pre_act)[1]
        gathered, act_seq, slope = lax.optimization_barrier((gathered, act_seq, slope))

        cut = hidden // 2 // 128 * 128
        spans = [(0, cut), (cut, hidden)] if cut else [(0, hidden)]
        summed = []
        for lo, hi in spans:
            term = jnp.einsum("so,ho->sh", gathered, w_out[lo:hi], preferred_element_type=jnp.float32)
            term = rows_of(term.astype(jnp.bfloat16), positions)
            summed.append(line_sum(term, me, n_tile, local_rows))
        weight_term = jnp.einsum("sh,so->ho", act_seq, gathered, preferred_element_type=jnp.float32)
        local_sum = jnp.sum(gathered, axis=0, dtype=jnp.float32)
        grad_pre = jnp.concatenate(summed, axis=1) * slope
        return (grad_pre, weight_term, local_sum)

    in_specs = (P("text", "tile"), P(), P("tile", "text"), P("text", "tile"))
    out_specs = (P("tile", "text"), P("text", "tile"), P("tile"))
    return jax.shard_map(body, mesh=mesh, in_specs=in_specs, out_specs=out_specs, check_vma=False)
```

```python
import jax
import jax.numpy as jnp
from jax import lax
from jax.experimental import pallas as pl
from jax.experimental.pallas import tpu as pltpu
from jax.sharding import PartitionSpec as P


def gelu_parts(pre):
    value = pre.astype(jnp.float32)
    cdf = 0.5 * (1.0 + jax.scipy.special.erf(value * 0.7071067811865476))
    activated = value * cdf
    slope = cdf + value * jnp.exp(-0.5 * value * value) * 0.3989422804014327
    return (activated, slope)


def rows_of(table, index):
    return table.at[index].get(mode="promise_in_bounds", unique_indices=True)


def plane_kernel(g_ref, w_ref, full_ref, term_ref, held, weight, send_sem, recv_sem, own_sem, out_sem):
    t = lax.axis_index("text")
    core, x, y = t % 2, t // 2 % 2, t // 4
    across, beside, above = 1 - 2 * core, 2 - 4 * x, 4 - 8 * y
    mate, xn, yn = t + across, t + beside, t + above
    diag = t + beside + above
    rows = g_ref.shape[0]
    half = rows // 2

    def part(owner, k):
        return pl.ds(pl.multiple_of(owner * rows + k * half, 16), half)

    barrier = pltpu.get_barrier_semaphore()
    for other in (mate, xn, yn):
        pl.semaphore_signal(barrier, inc=1, device_id={"text": other}, device_id_type=pl.DeviceIdType.MESH)
    pl.semaphore_wait(barrier, 3)

    count = [0]

    def send(src, dst, other):
        k = count[0]
        count[0] += 1
        copy = pltpu.make_async_remote_copy(
            src_ref=src, dst_ref=held.at[dst], send_sem=send_sem.at[k], recv_sem=recv_sem.at[k],
            device_id={"text": other}, device_id_type=pl.DeviceIdType.MESH)
        copy.start()
        return copy

    outs = []

    def use(owner, k):
        at = part(owner, k)
        out = pltpu.make_async_copy(held.at[at], full_ref.at[at], out_sem.at[len(outs)])
        out.start()
        outs.append(out)
        term_ref[at, :] = lax.dot_general(
            held[at, :], weight[...], (((1,), (1,)), ((), ())),
            preferred_element_type=jnp.float32).astype(term_ref.dtype)

    def mine(k):
        return g_ref.at[pl.ds(k * half, half)]

    def pass_on(owner, k, other):
        return send(held.at[part(owner, k)], part(owner, k), other)

    x0 = send(mine(0), part(t, 0), xn)
    y0 = send(mine(1), part(t, 1), yn)
    x1 = send(mine(1), part(t, 1), xn)
    y1 = send(mine(0), part(t, 0), yn)
    m0 = send(mine(0), part(t, 0), mate)
    m1 = send(mine(1), part(t, 1), mate)
    own = [pltpu.make_async_copy(mine(k), held.at[part(t, k)], own_sem.at[k]) for k in range(2)]
    load = pltpu.make_async_copy(w_ref, weight, own_sem.at[2])
    load.start()
    for copy in own:
        copy.start()
    load.wait()
    for k in range(2):
        own[k].wait()
        use(t, k)
    m0.wait_recv()
    use(mate, 0)
    m1.wait_recv()
    use(mate, 1)

    x0.wait_recv()
    yf = pass_on(xn, 0, yn)
    mx0 = pass_on(xn, 0, mate)
    y0.wait_recv()
    xf = pass_on(yn, 1, xn)
    my0 = pass_on(yn, 1, mate)
    use(xn, 0)
    use(yn, 1)
    mx0.wait_recv()
    use(xn + across, 0)
    my0.wait_recv()
    use(yn + across, 1)

    x1.wait_recv()
    mx1 = pass_on(xn, 1, mate)
    y1.wait_recv()
    my1 = pass_on(yn, 0, mate)
    use(xn, 1)
    use(yn, 0)
    mx1.wait_recv()
    use(xn + across, 1)
    my1.wait_recv()
    use(yn + across, 0)

    yf.wait_recv()
    md0 = pass_on(diag, 0, mate)
    xf.wait_recv()
    md1 = pass_on(diag, 1, mate)
    use(diag, 0)
    use(diag, 1)
    md0.wait_recv()
    use(diag + across, 0)
    md1.wait_recv()
    use(diag + across, 1)

    for copy in (x0, y0, x1, y1, m0, m1, yf, mx0, xf, my0, mx1, my1, md0, md1):
        copy.wait_send()
    for out in outs:
        out.wait()


def plane_gather(grad_seq, w_out, n_text):
    rows, columns = grad_seq.shape
    hidden = w_out.shape[0]
    slots = rows * n_text
    anywhere = pl.BlockSpec(memory_space=pl.ANY)
    return pl.pallas_call(
        plane_kernel,
        out_shape=(jax.ShapeDtypeStruct((slots, columns), jnp.bfloat16),
                   jax.ShapeDtypeStruct((slots, hidden), jnp.bfloat16)),
        in_specs=[anywhere, anywhere],
        out_specs=(anywhere, pl.BlockSpec(memory_space=pltpu.VMEM)),
        scratch_shapes=[
            pltpu.VMEM((slots, columns), jnp.bfloat16),
            pltpu.VMEM((hidden, columns), jnp.bfloat16),
            pltpu.SemaphoreType.DMA((14,)),
            pltpu.SemaphoreType.DMA((14,)),
            pltpu.SemaphoreType.DMA((3,)),
            pltpu.SemaphoreType.DMA((2 * n_text,)),
        ],
        compiler_params=pltpu.CompilerParams(
            collective_id=0, has_side_effects=True, vmem_limit_bytes=40 * 2**20),
        cost_estimate=pl.CostEstimate(
            flops=2 * slots * hidden * columns, bytes_accessed=60 * 2**20, transcendentals=0),
    )(grad_seq, w_out)


def line_sum(term, me, n, rows):
    def mine(block):
        start = jnp.clip(block, 0, n - 1) * rows
        return lax.dynamic_slice_in_dim(term, start, rows, 0).astype(jnp.float32)

    total = mine(me)
    right = left = None
    for step in range(1, n):
        ahead = n - step
        out_right, out_left = mine(me + ahead), mine(me - ahead)
        if right is not None:
            out_right = out_right + right.astype(jnp.float32)
            out_left = out_left + left.astype(jnp.float32)
        hops = range(min(step, n - 1))
        right = lax.ppermute(out_right.astype(jnp.bfloat16), "tile", [(i, i + 1) for i in hops])
        left = lax.ppermute(out_left.astype(jnp.bfloat16), "tile", [(n - 1 - i, n - 2 - i) for i in hops])
    return total + right.astype(jnp.float32) + left.astype(jnp.float32)


def solution(mesh):
    n_tile, n_text = mesh.shape["tile"], mesh.shape["text"]

    def body(grad_seq, positions, pre_act, w_out):
        local_rows, hidden = pre_act.shape
        slots = positions.shape[0]
        me = lax.axis_index("tile")
        if n_text == 8:
            gathered, term = plane_gather(grad_seq, w_out, n_text)
        else:
            gathered = lax.all_gather(grad_seq, "text", axis=0, tiled=True)
            term = jnp.einsum(
                "so,ho->sh", gathered, w_out, preferred_element_type=jnp.float32).astype(jnp.bfloat16)

        blocks = [pre_act]
        for shift in range(1, n_tile):
            ring = [(i, (i + shift) % n_tile) for i in range(n_tile)]
            blocks.append(lax.ppermute(pre_act, "tile", ring))
        blocks = lax.optimization_barrier((blocks, term))[0]
        slot = jnp.arange(slots, dtype=jnp.int32)
        turned = (me - slot // local_rows) % n_tile * local_rows + slot % local_rows
        source = jnp.zeros((slots,), jnp.int32).at[positions].set(
            turned, mode="promise_in_bounds", unique_indices=True)
        act = jnp.concatenate([gelu_parts(b)[0].astype(jnp.bfloat16) for b in blocks], axis=0)
        act_seq = rows_of(act, source)
        slope = gelu_parts(pre_act)[1]

        cut = hidden // 2 // 128 * 128
        spans = [(0, cut), (cut, hidden)] if cut else [(0, hidden)]
        summed = []
        for lo, hi in spans:
            summed.append(line_sum(rows_of(term[:, lo:hi], positions), me, n_tile, local_rows))
        weight_term = jnp.einsum("sh,so->ho", act_seq, gathered, preferred_element_type=jnp.float32)
        local_sum = jnp.sum(gathered, axis=0, dtype=jnp.float32)
        grad_pre = jnp.concatenate(summed, axis=1) * slope
        return (grad_pre, weight_term, local_sum)

    in_specs = (P("text", "tile"), P(), P("tile", "text"), P("text", "tile"))
    out_specs = (P("tile", "text"), P("text", "tile"), P("tile"))
    return jax.shard_map(body, mesh=mesh, in_specs=in_specs, out_specs=out_specs, check_vma=False)
```

```python
import jax
import jax.numpy as jnp
from jax import lax
from jax.experimental import pallas as pl
from jax.experimental.pallas import tpu as pltpu
from jax.sharding import PartitionSpec as P


def gelu_parts(pre):
    value = pre.astype(jnp.float32)
    cdf = 0.5 * (1.0 + jax.scipy.special.erf(value * 0.7071067811865476))
    activated = value * cdf
    slope = cdf + value * jnp.exp(-0.5 * value * value) * 0.3989422804014327
    return (activated, slope)


def rows_of(table, index):
    return table.at[index].get(mode="promise_in_bounds", unique_indices=True)


def plane_kernel(g_ref, w_ref, full_ref, term_ref, held, weight, send_sem, recv_sem, own_sem, out_sem):
    t = lax.axis_index("text")
    core, x, y = t % 2, t // 2 % 2, t // 4
    across, beside, above = 1 - 2 * core, 2 - 4 * x, 4 - 8 * y
    mate, xn, yn = t + across, t + beside, t + above
    diag = t + beside + above
    rows = g_ref.shape[0]
    half = rows // 2

    def part(owner, k):
        return pl.ds(pl.multiple_of(owner * rows + k * half, 16), half)

    barrier = pltpu.get_barrier_semaphore()
    for other in (mate, xn, yn):
        pl.semaphore_signal(barrier, inc=1, device_id={"text": other}, device_id_type=pl.DeviceIdType.MESH)
    pl.semaphore_wait(barrier, 3)

    count = [0]

    def send(src, dst, other):
        k = count[0]
        count[0] += 1
        copy = pltpu.make_async_remote_copy(
            src_ref=src, dst_ref=held.at[dst], send_sem=send_sem.at[k], recv_sem=recv_sem.at[k],
            device_id={"text": other}, device_id_type=pl.DeviceIdType.MESH)
        copy.start()
        return copy

    outs = []

    def use(owner, k):
        at = part(owner, k)
        out = pltpu.make_async_copy(held.at[at], full_ref.at[at], out_sem.at[len(outs)])
        out.start()
        outs.append(out)
        term_ref[at, :] = lax.dot_general(
            held[at, :], weight[...], (((1,), (1,)), ((), ())),
            preferred_element_type=jnp.float32).astype(term_ref.dtype)

    def mine(k):
        return g_ref.at[pl.ds(k * half, half)]

    def pass_on(owner, k, other):
        return send(held.at[part(owner, k)], part(owner, k), other)

    x0 = send(mine(0), part(t, 0), xn)
    y0 = send(mine(1), part(t, 1), yn)
    x1 = send(mine(1), part(t, 1), xn)
    y1 = send(mine(0), part(t, 0), yn)
    m0 = send(mine(0), part(t, 0), mate)
    m1 = send(mine(1), part(t, 1), mate)
    own = [pltpu.make_async_copy(mine(k), held.at[part(t, k)], own_sem.at[k]) for k in range(2)]
    load = pltpu.make_async_copy(w_ref, weight, own_sem.at[2])
    load.start()
    for copy in own:
        copy.start()
    load.wait()
    for k in range(2):
        own[k].wait()
        use(t, k)
    m0.wait_recv()
    use(mate, 0)
    m1.wait_recv()
    use(mate, 1)

    x0.wait_recv()
    yf = pass_on(xn, 0, yn)
    mx0 = pass_on(xn, 0, mate)
    y0.wait_recv()
    xf = pass_on(yn, 1, xn)
    my0 = pass_on(yn, 1, mate)
    use(xn, 0)
    use(yn, 1)
    mx0.wait_recv()
    use(xn + across, 0)
    my0.wait_recv()
    use(yn + across, 1)

    x1.wait_recv()
    mx1 = pass_on(xn, 1, mate)
    y1.wait_recv()
    my1 = pass_on(yn, 0, mate)
    use(xn, 1)
    use(yn, 0)
    mx1.wait_recv()
    use(xn + across, 1)
    my1.wait_recv()
    use(yn + across, 0)

    yf.wait_recv()
    md0 = pass_on(diag, 0, mate)
    xf.wait_recv()
    md1 = pass_on(diag, 1, mate)
    use(diag, 0)
    use(diag, 1)
    md0.wait_recv()
    use(diag + across, 0)
    md1.wait_recv()
    use(diag + across, 1)

    for copy in (x0, y0, x1, y1, m0, m1, yf, mx0, xf, my0, mx1, my1, md0, md1):
        copy.wait_send()
    for out in outs:
        out.wait()


def plane_gather(grad_seq, w_out, n_text):
    rows, columns = grad_seq.shape
    hidden = w_out.shape[0]
    slots = rows * n_text
    anywhere = pl.BlockSpec(memory_space=pl.ANY)
    return pl.pallas_call(
        plane_kernel,
        out_shape=(jax.ShapeDtypeStruct((slots, columns), jnp.bfloat16),
                   jax.ShapeDtypeStruct((slots, hidden), jnp.bfloat16)),
        in_specs=[anywhere, anywhere],
        out_specs=(anywhere, pl.BlockSpec(memory_space=pltpu.VMEM)),
        scratch_shapes=[
            pltpu.VMEM((slots, columns), jnp.bfloat16),
            pltpu.VMEM((hidden, columns), jnp.bfloat16),
            pltpu.SemaphoreType.DMA((14,)),
            pltpu.SemaphoreType.DMA((14,)),
            pltpu.SemaphoreType.DMA((3,)),
            pltpu.SemaphoreType.DMA((2 * n_text,)),
        ],
        compiler_params=pltpu.CompilerParams(
            collective_id=0, has_side_effects=True, vmem_limit_bytes=40 * 2**20),
        cost_estimate=pl.CostEstimate(
            flops=2 * slots * hidden * columns, bytes_accessed=60 * 2**20, transcendentals=0),
    )(grad_seq, w_out)


def line_kernel(n, subs, width, term_ref, pre_refs, place_ref, full_ref, grad_ref, weight_ref, bias_ref,
                act, turned, full, out, arrive, leave, send_sem, recv_sem, load_sem, out_sem):
    me = lax.axis_index("tile")
    rows, hidden = pre_refs[0].shape
    slots, columns = full_ref.shape
    size = rows // subs
    mesh_ids = pl.DeviceIdType.MESH
    barrier = pltpu.get_barrier_semaphore()

    for other in ((me + 1) % n, (me + n - 1) % n):
        pl.semaphore_signal(barrier, inc=1, device_id={"tile": other}, device_id_type=mesh_ids)
    pl.semaphore_wait(barrier, 2)

    load = pltpu.make_async_copy(full_ref, full, load_sem)
    load.start()

    def hop(way, step, j, src):
        k = ((way * (n - 1)) + step - 1) * subs + j
        return pltpu.make_async_remote_copy(
            src_ref=src, dst_ref=arrive.at[way, step - 1, pl.ds(j * size, size)],
            send_sem=send_sem.at[k], recv_sem=recv_sem.at[k],
            device_id={"tile": me + 1 - 2 * way}, device_id_type=mesh_ids)

    def place(way):
        return me if way == 0 else n - 1 - me

    def poll(step, j):
        piece = pl.ds(j * size, size)
        for way in range(2):
            i = place(way)

            def own():
                block = me + n - step if way == 0 else me - n + step
                return pl.ds(pl.multiple_of(block * rows + j * size, 16), size)

            @pl.when(i == 0)
            def _():
                hop(way, step, j, term_ref.at[own()]).start()

            if step > 1:
                @pl.when((i >= 1) & (i <= step - 1))
                def _():
                    hop(way, step - 1, j, leave.at[way, step - 2, piece]).wait_recv()
                    total = (term_ref[own(), :].astype(jnp.float32)
                             + arrive[way, step - 2, piece, :].astype(jnp.float32))
                    leave[way, step - 1, piece, :] = total.astype(jnp.bfloat16)
                    hop(way, step, j, leave.at[way, step - 1, piece]).start()

    def last(j):
        piece = pl.ds(j * size, size)
        for way in range(2):
            @pl.when(place(way) >= 1)
            def _():
                hop(way, n - 1, j, leave.at[way, n - 2, piece]).wait_recv()
        own = pl.ds(pl.multiple_of(me * rows + j * size, 16), size)
        chunk = 32
        inside_right, inside_left = me > 0, me < n - 1

        def finish(c, carry):
            at = pl.ds(pl.multiple_of(j * size + c * chunk, 16), chunk)
            total = term_ref[pl.ds(pl.multiple_of(me * rows + j * size + c * chunk, 16), chunk), :].astype(jnp.float32)
            right = arrive[0, n - 2, at, :].astype(jnp.float32)
            left = arrive[1, n - 2, at, :].astype(jnp.float32)
            total = total + jnp.where(inside_right, right, 0.0) + jnp.where(inside_left, left, 0.0)
            grad_ref[at, :] = total * gelu_parts(pre_refs[0][at, :])[1]
            return carry

        lax.fori_loop(0, size // chunk, finish, 0)

    def activate(k):
        chunk = 32

        def run(c, carry):
            at = pl.ds(pl.multiple_of(c * chunk, chunk), chunk)
            to = pl.ds(pl.multiple_of(k * rows + c * chunk, chunk), chunk)
            act[to, :] = gelu_parts(pre_refs[k][at, :])[0].astype(jnp.bfloat16)
            return carry

        lax.fori_loop(0, rows // chunk, run, 0)

    def reorder(first, count):
        def run(c, carry):
            start = pl.multiple_of(c * width, width)
            row = lax.broadcasted_iota(jnp.int32, (width, slots), 0) + start
            chosen = jnp.where(row == place_ref[...], 1.0, 0.0).astype(jnp.bfloat16)
            moved = lax.dot_general(chosen, act[...], (((1,), (0,)), ((), ())), preferred_element_type=jnp.float32)
            turned[:, pl.ds(start, width)] = moved.T.astype(jnp.bfloat16)
            return carry

        lax.fori_loop(first, first + count, run, 0)

    def weigh(first, count):
        def run(c, carry):
            at = pl.ds(pl.multiple_of(c * width, width), width)
            out[:, at] = jnp.dot(turned[...], full[:, at], preferred_element_type=jnp.float32)
            ones = jnp.ones((16, slots), jnp.bfloat16)
            bias_ref[:, at] = jnp.dot(ones, full[:, at], preferred_element_type=jnp.float32)[:1]
            return carry

        lax.fori_loop(first, first + count, run, 0)

    work = [lambda k=k: activate(k) for k in range(n)]
    work += [lambda c=c: reorder(c, 1) for c in range(slots // width)]
    work.append(load.wait)
    work += [lambda c=c: weigh(c, 1) for c in range(columns // width)]

    for j in range(subs):
        poll(1, j)
    gaps = (n - 1) * subs
    done = 0
    for g in range(gaps):
        upto = len(work) * (g + 1) // gaps
        for item in work[done:upto]:
            item()
        done = upto
        step, j = g // subs + 2, g % subs
        if g == gaps - 1:
            flush = pltpu.make_async_copy(out, weight_ref, out_sem)
            flush.start()
        if step < n:
            poll(step, j)
        else:
            last(j)
    flush.wait()
    for way in range(2):
        for step in range(1, n):
            @pl.when(place(way) <= step - 1)
            def _():
                for j in range(subs):
                    hop(way, step, j, leave.at[way, step - 1, pl.ds(j * size, size)]).wait_send()


def line_finish(n, term, blocks, places, gathered):
    rows, hidden = blocks[0].shape
    slots, columns = gathered.shape
    subs, width = 4, 256
    anywhere, vmem = pl.BlockSpec(memory_space=pl.ANY), pl.BlockSpec(memory_space=pltpu.VMEM)

    def kernel(*refs):
        line_kernel(n, subs, width, refs[0], refs[1:n + 1], *refs[n + 1:])

    count = 2 * (n - 1) * subs
    return pl.pallas_call(
        kernel,
        out_shape=(jax.ShapeDtypeStruct((rows, hidden), jnp.float32),
                   jax.ShapeDtypeStruct((hidden, columns), jnp.float32),
                   jax.ShapeDtypeStruct((1, columns), jnp.float32)),
        in_specs=[vmem] * (n + 2) + [anywhere],
        out_specs=(vmem, anywhere, vmem),
        scratch_shapes=[
            pltpu.VMEM((slots, hidden), jnp.bfloat16),
            pltpu.VMEM((hidden, slots), jnp.bfloat16),
            pltpu.VMEM((slots, columns), jnp.bfloat16),
            pltpu.VMEM((hidden, columns), jnp.float32),
            pltpu.VMEM((2, n - 1, rows, hidden), jnp.bfloat16),
            pltpu.VMEM((2, n - 1, rows, hidden), jnp.bfloat16),
            pltpu.SemaphoreType.DMA((count,)),
            pltpu.SemaphoreType.DMA((count,)),
            pltpu.SemaphoreType.DMA,
            pltpu.SemaphoreType.DMA,
        ],
        compiler_params=pltpu.CompilerParams(
            collective_id=1, has_side_effects=True, vmem_limit_bytes=60 * 2**20),
    )(term, *blocks, places, gathered)


def line_sum(term, me, n, rows):
    def mine(block):
        start = jnp.clip(block, 0, n - 1) * rows
        return lax.dynamic_slice_in_dim(term, start, rows, 0).astype(jnp.float32)

    total = mine(me)
    right = left = None
    for step in range(1, n):
        ahead = n - step
        out_right, out_left = mine(me + ahead), mine(me - ahead)
        if right is not None:
            out_right = out_right + right.astype(jnp.float32)
            out_left = out_left + left.astype(jnp.float32)
        hops = range(min(step, n - 1))
        right = lax.ppermute(out_right.astype(jnp.bfloat16), "tile", [(i, i + 1) for i in hops])
        left = lax.ppermute(out_left.astype(jnp.bfloat16), "tile", [(n - 1 - i, n - 2 - i) for i in hops])
    return total + right.astype(jnp.float32) + left.astype(jnp.float32)


def solution(mesh):
    n_tile, n_text = mesh.shape["tile"], mesh.shape["text"]

    def body(grad_seq, positions, pre_act, w_out):
        local_rows, hidden = pre_act.shape
        slots = positions.shape[0]
        me = lax.axis_index("tile")
        if n_text == 8:
            gathered, term = plane_gather(grad_seq, w_out, n_text)
        else:
            gathered = lax.all_gather(grad_seq, "text", axis=0, tiled=True)
            term = jnp.einsum(
                "so,ho->sh", gathered, w_out, preferred_element_type=jnp.float32).astype(jnp.bfloat16)

        blocks = [pre_act]
        for shift in range(1, n_tile):
            ring = [(i, (i + shift) % n_tile) for i in range(n_tile)]
            blocks.append(lax.ppermute(pre_act, "tile", ring))
        if n_text == 8:
            tiles = [(me - k) % n_tile for k in range(n_tile)]
            places = jnp.concatenate([
                lax.dynamic_slice_in_dim(positions, t * local_rows, local_rows) for t in tiles]).reshape(1, slots)
            grad_pre, weight_term, bias = line_finish(
                n_tile, rows_of(term, positions), blocks, places, gathered)
            return (grad_pre, weight_term, bias.reshape(-1))
        blocks = lax.optimization_barrier((blocks, term))[0]
        slot = jnp.arange(slots, dtype=jnp.int32)
        turned = (me - slot // local_rows) % n_tile * local_rows + slot % local_rows
        source = jnp.zeros((slots,), jnp.int32).at[positions].set(
            turned, mode="promise_in_bounds", unique_indices=True)
        act = jnp.concatenate([gelu_parts(b)[0].astype(jnp.bfloat16) for b in blocks], axis=0)
        act_seq = rows_of(act, source)
        slope = gelu_parts(pre_act)[1]

        cut = hidden // 2 // 128 * 128
        spans = [(0, cut), (cut, hidden)] if cut else [(0, hidden)]
        summed = []
        for lo, hi in spans:
            summed.append(line_sum(rows_of(term[:, lo:hi], positions), me, n_tile, local_rows))
        weight_term = jnp.einsum("sh,so->ho", act_seq, gathered, preferred_element_type=jnp.float32)
        local_sum = jnp.sum(gathered, axis=0, dtype=jnp.float32)
        grad_pre = jnp.concatenate(summed, axis=1) * slope
        return (grad_pre, weight_term, local_sum)

    in_specs = (P("text", "tile"), P(), P("tile", "text"), P("text", "tile"))
    out_specs = (P("tile", "text"), P("text", "tile"), P("tile"))
    return jax.shard_map(body, mesh=mesh, in_specs=in_specs, out_specs=out_specs, check_vma=False)
```

```python
import jax
import jax.numpy as jnp
from jax import lax
from jax.experimental import pallas as pl
from jax.experimental.pallas import tpu as pltpu
from jax.sharding import PartitionSpec as P


def gelu_parts(pre):
    value = pre.astype(jnp.float32)
    cdf = 0.5 * (1.0 + jax.scipy.special.erf(value * 0.7071067811865476))
    activated = value * cdf
    slope = cdf + value * jnp.exp(-0.5 * value * value) * 0.3989422804014327
    return (activated, slope)


def rows_of(table, index):
    return table.at[index].get(mode="promise_in_bounds", unique_indices=True)


def plane_kernel(g_ref, w_ref, full_ref, term_ref, held, weight, send_sem, recv_sem, own_sem, out_sem):
    t = lax.axis_index("text")
    core, x, y = t % 2, t // 2 % 2, t // 4
    across, beside, above = 1 - 2 * core, 2 - 4 * x, 4 - 8 * y
    mate, xn, yn = t + across, t + beside, t + above
    diag = t + beside + above
    rows = g_ref.shape[0]
    half = rows // 2

    def part(owner, k):
        return pl.ds(pl.multiple_of(owner * rows + k * half, 16), half)

    barrier = pltpu.get_barrier_semaphore()
    for other in (mate, xn, yn):
        pl.semaphore_signal(barrier, inc=1, device_id={"text": other}, device_id_type=pl.DeviceIdType.MESH)
    pl.semaphore_wait(barrier, 3)

    count = [0]

    def send(src, dst, other):
        k = count[0]
        count[0] += 1
        copy = pltpu.make_async_remote_copy(
            src_ref=src, dst_ref=held.at[dst], send_sem=send_sem.at[k], recv_sem=recv_sem.at[k],
            device_id={"text": other}, device_id_type=pl.DeviceIdType.MESH)
        copy.start()
        return copy

    outs = []

    def use(owner, k):
        at = part(owner, k)
        out = pltpu.make_async_copy(held.at[at], full_ref.at[at], out_sem.at[len(outs)])
        out.start()
        outs.append(out)
        term_ref[at, :] = lax.dot_general(
            held[at, :], weight[...], (((1,), (1,)), ((), ())),
            preferred_element_type=jnp.float32).astype(term_ref.dtype)

    def mine(k):
        return g_ref.at[pl.ds(k * half, half)]

    def pass_on(owner, k, other):
        return send(held.at[part(owner, k)], part(owner, k), other)

    x0 = send(mine(0), part(t, 0), xn)
    y0 = send(mine(1), part(t, 1), yn)
    x1 = send(mine(1), part(t, 1), xn)
    y1 = send(mine(0), part(t, 0), yn)
    m0 = send(mine(0), part(t, 0), mate)
    m1 = send(mine(1), part(t, 1), mate)
    own = [pltpu.make_async_copy(mine(k), held.at[part(t, k)], own_sem.at[k]) for k in range(2)]
    load = pltpu.make_async_copy(w_ref, weight, own_sem.at[2])
    load.start()
    for copy in own:
        copy.start()
    load.wait()
    for k in range(2):
        own[k].wait()
        use(t, k)
    m0.wait_recv()
    use(mate, 0)
    m1.wait_recv()
    use(mate, 1)

    x0.wait_recv()
    yf = pass_on(xn, 0, yn)
    mx0 = pass_on(xn, 0, mate)
    y0.wait_recv()
    xf = pass_on(yn, 1, xn)
    my0 = pass_on(yn, 1, mate)
    use(xn, 0)
    use(yn, 1)
    mx0.wait_recv()
    use(xn + across, 0)
    my0.wait_recv()
    use(yn + across, 1)

    x1.wait_recv()
    mx1 = pass_on(xn, 1, mate)
    y1.wait_recv()
    my1 = pass_on(yn, 0, mate)
    use(xn, 1)
    use(yn, 0)
    mx1.wait_recv()
    use(xn + across, 1)
    my1.wait_recv()
    use(yn + across, 0)

    yf.wait_recv()
    md0 = pass_on(diag, 0, mate)
    xf.wait_recv()
    md1 = pass_on(diag, 1, mate)
    use(diag, 0)
    use(diag, 1)
    md0.wait_recv()
    use(diag + across, 0)
    md1.wait_recv()
    use(diag + across, 1)

    for copy in (x0, y0, x1, y1, m0, m1, yf, mx0, xf, my0, mx1, my1, md0, md1):
        copy.wait_send()
    for out in outs:
        out.wait()


def plane_gather(grad_seq, w_out, n_text):
    rows, columns = grad_seq.shape
    hidden = w_out.shape[0]
    slots = rows * n_text
    anywhere = pl.BlockSpec(memory_space=pl.ANY)
    return pl.pallas_call(
        plane_kernel,
        out_shape=(jax.ShapeDtypeStruct((slots, columns), jnp.bfloat16),
                   jax.ShapeDtypeStruct((slots, hidden), jnp.bfloat16)),
        in_specs=[anywhere, anywhere],
        out_specs=(anywhere, pl.BlockSpec(memory_space=pltpu.VMEM)),
        scratch_shapes=[
            pltpu.VMEM((slots, columns), jnp.bfloat16),
            pltpu.VMEM((hidden, columns), jnp.bfloat16),
            pltpu.SemaphoreType.DMA((14,)),
            pltpu.SemaphoreType.DMA((14,)),
            pltpu.SemaphoreType.DMA((3,)),
            pltpu.SemaphoreType.DMA((2 * n_text,)),
        ],
        compiler_params=pltpu.CompilerParams(
            collective_id=0, has_side_effects=True, vmem_limit_bytes=60 * 2**20),
        cost_estimate=pl.CostEstimate(
            flops=2 * slots * hidden * columns, bytes_accessed=60 * 2**20, transcendentals=0),
    )(grad_seq, w_out)


def line_kernel(n, subs, width, term_ref, pre_refs, place_ref, full_ref, grad_ref, weight_ref, bias_ref,
                act, turned, full, arrive, leave, send_sem, recv_sem, load_sem):
    me = lax.axis_index("tile")
    rows, hidden = pre_refs[0].shape
    slots, columns = full_ref.shape
    size = rows // subs
    mesh_ids = pl.DeviceIdType.MESH
    barrier = pltpu.get_barrier_semaphore()

    for other in ((me + 1) % n, (me + n - 1) % n):
        pl.semaphore_signal(barrier, inc=1, device_id={"tile": other}, device_id_type=mesh_ids)
    pl.semaphore_wait(barrier, 2)

    load = pltpu.make_async_copy(full_ref, full, load_sem)
    load.start()

    def hop(way, step, j, src):
        k = ((way * (n - 1)) + step - 1) * subs + j
        return pltpu.make_async_remote_copy(
            src_ref=src, dst_ref=arrive.at[way, step - 1, pl.ds(j * size, size)],
            send_sem=send_sem.at[k], recv_sem=recv_sem.at[k],
            device_id={"tile": me + 1 - 2 * way}, device_id_type=mesh_ids)

    def place(way):
        return me if way == 0 else n - 1 - me

    def poll(step, j):
        piece = pl.ds(j * size, size)
        for way in range(2):
            i = place(way)

            def own():
                block = me + n - step if way == 0 else me - n + step
                return pl.ds(pl.multiple_of(block * rows + j * size, 16), size)

            @pl.when(i == 0)
            def _():
                hop(way, step, j, term_ref.at[own()]).start()

            if step > 1:
                @pl.when((i >= 1) & (i <= step - 1))
                def _():
                    hop(way, step - 1, j, leave.at[way, step - 2, piece]).wait_recv()
                    total = (term_ref[own(), :].astype(jnp.float32)
                             + arrive[way, step - 2, piece, :].astype(jnp.float32))
                    leave[way, step - 1, piece, :] = total.astype(jnp.bfloat16)
                    hop(way, step, j, leave.at[way, step - 1, piece]).start()

    def last(j):
        piece = pl.ds(j * size, size)
        for way in range(2):
            @pl.when(place(way) >= 1)
            def _():
                hop(way, n - 1, j, leave.at[way, n - 2, piece]).wait_recv()
        own = pl.ds(pl.multiple_of(me * rows + j * size, 16), size)
        chunk = 32
        inside_right, inside_left = me > 0, me < n - 1

        def finish(c, carry):
            at = pl.ds(pl.multiple_of(j * size + c * chunk, 16), chunk)
            total = term_ref[pl.ds(pl.multiple_of(me * rows + j * size + c * chunk, 16), chunk), :].astype(jnp.float32)
            right = arrive[0, n - 2, at, :].astype(jnp.float32)
            left = arrive[1, n - 2, at, :].astype(jnp.float32)
            total = total + jnp.where(inside_right, right, 0.0) + jnp.where(inside_left, left, 0.0)
            grad_ref[at, :] = total * gelu_parts(pre_refs[0][at, :])[1]
            return carry

        lax.fori_loop(0, size // chunk, finish, 0)

    def activate(k):
        chunk = 32

        def run(c, carry):
            at = pl.ds(pl.multiple_of(c * chunk, chunk), chunk)
            to = pl.ds(pl.multiple_of(k * rows + c * chunk, chunk), chunk)
            act[to, :] = gelu_parts(pre_refs[k][at, :])[0].astype(jnp.bfloat16)
            return carry

        lax.fori_loop(0, rows // chunk, run, 0)

    def reorder(first, count):
        def run(c, carry):
            start = pl.multiple_of(c * width, width)
            row = lax.broadcasted_iota(jnp.int32, (width, slots), 0) + start
            chosen = jnp.where(row == place_ref[...], 1.0, 0.0).astype(jnp.bfloat16)
            moved = lax.dot_general(chosen, act[...], (((1,), (0,)), ((), ())), preferred_element_type=jnp.float32)
            turned[:, pl.ds(start, width)] = moved.T.astype(jnp.bfloat16)
            return carry

        lax.fori_loop(first, first + count, run, 0)

    def weigh(first, count):
        def run(c, carry):
            at = pl.ds(pl.multiple_of(c * width, width), width)
            weight_ref[:, at] = jnp.dot(turned[...], full[:, at], preferred_element_type=jnp.float32)
            ones = jnp.ones((16, slots), jnp.bfloat16)
            bias_ref[:, at] = jnp.dot(ones, full[:, at], preferred_element_type=jnp.float32)[:1]
            return carry

        lax.fori_loop(first, first + count, run, 0)

    work = [lambda k=k: activate(k) for k in range(n)]
    work += [lambda c=c: reorder(c, 1) for c in range(slots // width)]
    work.append(load.wait)
    work += [lambda c=c: weigh(c, 1) for c in range(columns // width)]

    for j in range(subs):
        poll(1, j)
    gaps = (n - 1) * subs
    done = 0
    for g in range(gaps):
        upto = len(work) * (g + 1) // gaps
        for item in work[done:upto]:
            item()
        done = upto
        step, j = g // subs + 2, g % subs
        if step < n:
            poll(step, j)
        else:
            last(j)
    for way in range(2):
        for step in range(1, n):
            @pl.when(place(way) <= step - 1)
            def _():
                for j in range(subs):
                    hop(way, step, j, leave.at[way, step - 1, pl.ds(j * size, size)]).wait_send()


def line_finish(n, term, blocks, places, gathered):
    rows, hidden = blocks[0].shape
    slots, columns = gathered.shape
    subs, width = 4, 256
    anywhere, vmem = pl.BlockSpec(memory_space=pl.ANY), pl.BlockSpec(memory_space=pltpu.VMEM)

    def kernel(*refs):
        line_kernel(n, subs, width, refs[0], refs[1:n + 1], *refs[n + 1:])

    count = 2 * (n - 1) * subs
    return pl.pallas_call(
        kernel,
        out_shape=(jax.ShapeDtypeStruct((rows, hidden), jnp.float32),
                   jax.ShapeDtypeStruct((hidden, columns), jnp.float32),
                   jax.ShapeDtypeStruct((1, columns), jnp.float32)),
        in_specs=[vmem] * (n + 2) + [anywhere],
        out_specs=(vmem, vmem, vmem),
        scratch_shapes=[
            pltpu.VMEM((slots, hidden), jnp.bfloat16),
            pltpu.VMEM((hidden, slots), jnp.bfloat16),
            pltpu.VMEM((slots, columns), jnp.bfloat16),
            pltpu.VMEM((2, n - 1, rows, hidden), jnp.bfloat16),
            pltpu.VMEM((2, n - 1, rows, hidden), jnp.bfloat16),
            pltpu.SemaphoreType.DMA((count,)),
            pltpu.SemaphoreType.DMA((count,)),
            pltpu.SemaphoreType.DMA,
        ],
        compiler_params=pltpu.CompilerParams(
            collective_id=1, has_side_effects=True, vmem_limit_bytes=40 * 2**20),
    )(term, *blocks, places, gathered)


def line_sum(term, me, n, rows):
    def mine(block):
        start = jnp.clip(block, 0, n - 1) * rows
        return lax.dynamic_slice_in_dim(term, start, rows, 0).astype(jnp.float32)

    total = mine(me)
    right = left = None
    for step in range(1, n):
        ahead = n - step
        out_right, out_left = mine(me + ahead), mine(me - ahead)
        if right is not None:
            out_right = out_right + right.astype(jnp.float32)
            out_left = out_left + left.astype(jnp.float32)
        hops = range(min(step, n - 1))
        right = lax.ppermute(out_right.astype(jnp.bfloat16), "tile", [(i, i + 1) for i in hops])
        left = lax.ppermute(out_left.astype(jnp.bfloat16), "tile", [(n - 1 - i, n - 2 - i) for i in hops])
    return total + right.astype(jnp.float32) + left.astype(jnp.float32)


def solution(mesh):
    n_tile, n_text = mesh.shape["tile"], mesh.shape["text"]

    def body(grad_seq, positions, pre_act, w_out):
        local_rows, hidden = pre_act.shape
        slots = positions.shape[0]
        me = lax.axis_index("tile")
        if n_text == 8:
            gathered, term = plane_gather(grad_seq, w_out, n_text)
        else:
            gathered = lax.all_gather(grad_seq, "text", axis=0, tiled=True)
            term = jnp.einsum(
                "so,ho->sh", gathered, w_out, preferred_element_type=jnp.float32).astype(jnp.bfloat16)

        blocks = [pre_act]
        for shift in range(1, n_tile):
            ring = [(i, (i + shift) % n_tile) for i in range(n_tile)]
            blocks.append(lax.ppermute(pre_act, "tile", ring))
        if n_text == 8:
            tiles = [(me - k) % n_tile for k in range(n_tile)]
            places = jnp.concatenate([
                lax.dynamic_slice_in_dim(positions, t * local_rows, local_rows) for t in tiles]).reshape(1, slots)
            grad_pre, weight_term, bias = line_finish(
                n_tile, rows_of(term, positions), blocks, places, gathered)
            return (grad_pre, weight_term, bias.reshape(-1))
        blocks = lax.optimization_barrier((blocks, term))[0]
        slot = jnp.arange(slots, dtype=jnp.int32)
        turned = (me - slot // local_rows) % n_tile * local_rows + slot % local_rows
        source = jnp.zeros((slots,), jnp.int32).at[positions].set(
            turned, mode="promise_in_bounds", unique_indices=True)
        act = jnp.concatenate([gelu_parts(b)[0].astype(jnp.bfloat16) for b in blocks], axis=0)
        act_seq = rows_of(act, source)
        slope = gelu_parts(pre_act)[1]

        cut = hidden // 2 // 128 * 128
        spans = [(0, cut), (cut, hidden)] if cut else [(0, hidden)]
        summed = []
        for lo, hi in spans:
            summed.append(line_sum(rows_of(term[:, lo:hi], positions), me, n_tile, local_rows))
        weight_term = jnp.einsum("sh,so->ho", act_seq, gathered, preferred_element_type=jnp.float32)
        local_sum = jnp.sum(gathered, axis=0, dtype=jnp.float32)
        grad_pre = jnp.concatenate(summed, axis=1) * slope
        return (grad_pre, weight_term, local_sum)

    in_specs = (P("text", "tile"), P(), P("tile", "text"), P("text", "tile"))
    out_specs = (P("tile", "text"), P("text", "tile"), P("tile"))
    return jax.shard_map(body, mesh=mesh, in_specs=in_specs, out_specs=out_specs, check_vma=False)
```
